32 devices in a mesh: groups: 2 (over x), seq: 16 (over z, y, core).
Axes of the slice: x: 2, y: 2, z: 4, core: 2. Of those that a mesh axis runs over, the one named last changes fastest.
Arguments:
- query: bfloat16 [2048, 4096], P(('groups', 'seq')), parts along dimension 0, may hold values from -28 to 28
- keys: bfloat16 [2048, 512], P(('groups', 'seq')), parts along dimension 0, may hold values from -4 to 4
- values: bfloat16 [2048, 512], P(('groups', 'seq')), parts along dimension 0, may hold values from -6 to 6
- query_bias: bfloat16 [4096], P('seq'), may hold values from -3 to 3
- key_bias: bfloat16 [512], P('seq'), may hold values from -3 to 3
- value_projection_bias: bfloat16 [512], P('seq'), may hold values from -3 to 3
- frame_order: int32 [128], P(('groups', 'seq')), parts along dimension 0, may hold values from 0 to 63, each once
Outputs:
- attended: bfloat16 [2048, 4096], P(('groups', 'seq')), parts along dimension 0
The draws below stay inside these ranges and needn't reach their ends.
There are 2 independent parts, one for each index of `groups`. The reference program is written for one: setup_inputs(seed, part) draws one part's arguments, and reference() takes and returns one part's arrays. A program takes and returns all parts, laid end to end along the dimension named above; an argument that names none is the same for every part. Nothing has to cross between parts.
Inputs may be any that keep to these rules, and one draw needn't show every extreme that they name: `frame_order`: each of the 64 frames stands in exactly one slot.
All inputs are finite; a program needn't handle non-finite values.
Results may differ from the reference program's by a relative error of at most 0.011.
Values may be sent and summed in bfloat16 or wider, within the bound.
A program may use at most 64 MiB of HBM per device.

```python
import math
import jax
import jax.numpy as jnp
from jax import lax

HEAD_SIZE = 128
QH = 32
KVH = 4
GRID = 4
FRAME_TOK = 16
FRAMES = 64
VISUAL_TOKENS = 1024


def draw_keys(key, part):
    result = jnp.clip(jax.random.normal(jax.random.fold_in(key, 13), (VISUAL_TOKENS, KVH * HEAD_SIZE), jnp.float32), -4.0, 4.0)
    return result.astype(jnp.bfloat16)


def draw_query(key, part):
    result = jnp.clip(jax.random.normal(jax.random.fold_in(key, 19), (VISUAL_TOKENS, QH * HEAD_SIZE), jnp.float32), -4.0, 4.0)
    return result.astype(jnp.bfloat16)


def block_scale(rng, shape, cuts, low, largest):
    loudness = 1.0
    for axis_at, blocks in cuts:
        draws = jax.random.uniform(jax.random.fold_in(jax.random.fold_in(rng, 6), axis_at), (blocks,), jnp.float32, low / len(cuts), largest / len(cuts))
        loudness = loudness * jnp.repeat(jnp.exp(draws), shape[axis_at] // blocks).reshape((-1,) + (1,) * (len(shape) - 1 - axis_at))
    return loudness


def scatter_about(stream_key, shape, deviation, reach, shards=(), held_as=jnp.bfloat16):
    values = deviation * jax.random.normal(stream_key, shape, jnp.float32)
    if shards:
        values = values * block_scale(stream_key, shape, shards, -0.22, 0.18)
    return jnp.clip(values, -reach, reach).astype(held_as)


def setup_inputs(seed: int = 0, part: int = 0) -> dict:
    key_list = jax.random.split(jax.random.key(seed), 8)
    part_splits = jax.random.split(jax.random.fold_in(key_list[7], part), 8)
    query = draw_query(jax.random.fold_in(jax.random.fold_in(key_list[7], part), 71), part)
    keys = draw_keys(jax.random.fold_in(jax.random.fold_in(key_list[7], part), 71), part)
    values = scatter_about(part_splits[2], (VISUAL_TOKENS, KVH * HEAD_SIZE), 1.0, 6.0, ((0, 16),))
    query_bias = scatter_about(key_list[3], (QH * HEAD_SIZE,), 0.5, 3.0, ((0, 16),))
    key_bias = scatter_about(key_list[4], (KVH * HEAD_SIZE,), 0.5, 3.0, ((0, 16),))
    value_projection_bias = scatter_about(key_list[5], (KVH * HEAD_SIZE,), 0.5, 3.0, ((0, 16),))
    frame_order = jax.random.permutation(part_splits[6], FRAMES).astype(jnp.int32)
    return {"query": query, "keys": keys, "values": values, "query_bias": query_bias, "key_bias": key_bias, "value_projection_bias": value_projection_bias, "frame_order": frame_order}


def positions(frame_order):
    count = frame_order.shape[0]
    within = jnp.tile(jnp.arange(FRAME_TOK, dtype=jnp.int32), count)
    return jnp.repeat(frame_order, FRAME_TOK) * FRAME_TOK + within

def rotate(matrix, gpos, heads):
    rows = matrix.shape[0]
    half = HEAD_SIZE // 2
    frame = gpos // FRAME_TOK
    within = gpos % FRAME_TOK
    temporal = (2 * frame).astype(matrix.dtype)
    vertical = (within // GRID).astype(matrix.dtype)
    lateral = (within % GRID).astype(matrix.dtype)
    pair = jnp.arange(half).astype(matrix.dtype)
    freq = jnp.exp(-(2.0 * pair / HEAD_SIZE) * math.log(1000000.0))
    source = jnp.where(pair[None, :] < half // 4, temporal[:, None], jnp.where(pair[None, :] < half // 4 + 3 * half // 8, vertical[:, None], lateral[:, None]))
    angle = source * freq[None, :]
    cosine = jnp.concatenate([jnp.cos(angle), jnp.cos(angle)], axis=1)[:, None, :]
    sine = jnp.concatenate([jnp.sin(angle), jnp.sin(angle)], axis=1)[:, None, :]
    shaped = matrix.reshape(rows, heads, HEAD_SIZE)
    turned = jnp.concatenate([-shaped[..., half:], shaped[..., :half]], axis=2)
    return (shaped * cosine + turned * sine).reshape(rows, heads * HEAD_SIZE)

def reference(query, keys, values, query_bias, key_bias, value_projection_bias, frame_order):
    gpos = positions(frame_order)
    qrot = rotate(query.astype(jnp.float32) + query_bias.astype(jnp.float32), gpos, QH).astype(jnp.bfloat16)
    krot = rotate(keys.astype(jnp.float32) + key_bias.astype(jnp.float32), gpos, KVH).astype(jnp.bfloat16)
    value_addend = (values.astype(jnp.float32) + value_projection_bias.astype(jnp.float32)).astype(jnp.bfloat16)
    ratio = QH // KVH
    scale = 1.0 / math.sqrt(HEAD_SIZE)
    qblock = math.gcd(VISUAL_TOKENS, 2048)
    qcount = VISUAL_TOKENS // qblock

    def one_head(head):
        query_group = head // ratio
        k_head = lax.dynamic_slice_in_dim(krot, (query_group * HEAD_SIZE).astype(jnp.int32), HEAD_SIZE, 1)
        value_head_slice = lax.dynamic_slice_in_dim(value_addend, (query_group * HEAD_SIZE).astype(jnp.int32), HEAD_SIZE, 1)

        def one_block(index):
            first = (index * qblock).astype(jnp.int32)
            q_rows = lax.dynamic_slice(qrot, (first, (head * HEAD_SIZE).astype(jnp.int32)), (qblock, HEAD_SIZE))
            q_pos = lax.dynamic_slice_in_dim(gpos, first, qblock)
            visible = gpos[None, :] <= q_pos[:, None]
            scores = jnp.dot(q_rows, k_head.T, preferred_element_type=jnp.float32) * scale
            top = lax.optimization_barrier(jnp.max(jnp.where(visible, scores, -1e+30), axis=1))
            expo = jnp.where(visible, jnp.exp(scores - top[:, None]), 0.0)
            den = lax.optimization_barrier(jnp.sum(expo, axis=1))
            mixed = jnp.dot(expo.astype(jnp.bfloat16), value_head_slice, preferred_element_type=jnp.float32)
            return (mixed / den[:, None]).astype(jnp.bfloat16)
        blocks = lax.map(one_block, jnp.arange(qcount, dtype=jnp.int32))
        return blocks.reshape(VISUAL_TOKENS, HEAD_SIZE)
    heads = lax.map(one_head, jnp.arange(QH, dtype=jnp.int32))
    return heads.transpose(1, 0, 2).reshape(VISUAL_TOKENS, QH * HEAD_SIZE)
```

```python
import functools
import math

import jax
import jax.numpy as jnp
import numpy as np
from jax import lax
from jax.experimental import pallas as pl
from jax.experimental.pallas import tpu as pltpu
from jax.sharding import PartitionSpec as P

HEAD = 128
HALF = HEAD // 2
QH = 32
KVH = 4
RATIO = QH // KVH
GRID = 4
FRAME_TOK = 16
MESH = pl.DeviceIdType.MESH
NEG = -1e30
PIECES = 2
PAIRS_T = HALF // 4
PAIRS_R = HALF // 4 + 3 * HALF // 8


def tables():
    pair = np.arange(HEAD) % HALF
    freq = np.exp(-(2.0 * pair / HEAD) * math.log(1000000.0))
    tok = np.arange(FRAME_TOK)
    source = np.where(pair[None, :] < PAIRS_R, (tok // GRID)[:, None], (tok % GRID)[:, None])
    angle = source * freq[None, :]
    sign = np.where(np.arange(HEAD) < HALF, -1.0, 1.0)
    rows = np.zeros((40, HEAD), np.float32)
    rows[0:16] = np.cos(angle)
    rows[16:32] = np.sin(angle) * sign[None, :]
    rows[32] = 2.0 * freq
    return rows


def cos_sin(frames, spatial):
    angle = frames * spatial[32:33, :]
    turns = jnp.round(angle * (1.0 / (2.0 * math.pi)))
    angle = angle - turns * 6.28125
    angle = angle - turns * (2.0 * math.pi - 6.28125)
    lane = lax.broadcasted_iota(jnp.int32, (FRAME_TOK, HEAD), 1)
    temporal = lane % HALF < PAIRS_T
    sign = jnp.where(lane < HALF, -1.0, 1.0)
    cos_t, sin_t = jnp.cos(angle), jnp.sin(angle)
    cosines, sines = [], []
    for j in range(frames.shape[0]):
        cosines.append(jnp.where(temporal, cos_t[j : j + 1, :], spatial[0:16, :]))
        sines.append(jnp.where(temporal, sin_t[j : j + 1, :] * sign, spatial[16:32, :]))
    return jnp.concatenate(cosines, axis=0), jnp.concatenate(sines, axis=0)


def spin(x, cosine, sine):
    return x * cosine + pltpu.roll(x, HALF, 1) * sine


def kernel(
    A, B, n, qper,
    q_hbm, k_hbm, v_hbm, qb_hbm, kb_hbm, vb_hbm, order_hbm, tab_hbm,
    o_ref,
    qb_ref, kb_ref, vb_ref, order_ref, tab_ref,
    q_ref, pack_ref, kbuf, vbuf, pbuf, qs, acc, top, den, ksc, vsc, hide,
    recv, send, precv, psend, load,
):
    me = lax.axis_index("seq")
    rows = kbuf.shape[1]
    frames = rows // FRAME_TOK
    cut = rows // (PIECES // 2)
    core = me % 2
    b = (me // 2) % B
    a = me // (2 * B)

    def piece(p, s):
        return (kbuf, vbuf)[p % 2].at[s, pl.ds((p // 2) * cut, cut)]

    def slot(x, y, z):
        return (x * B + y) * 2 + z

    ways = (
        (a + 1 < A, slot(a + 1, b, core)),
        (a > 0, slot(a - 1, b, core)),
        (b + 1 < B, slot(a, b + 1, core)),
        (b > 0, slot(a, b - 1, core)),
        (None, slot(a, b, 1 - core)),
    )

    def copy(t, s, way):
        return pltpu.make_async_remote_copy(
            src_ref=piece(t, s),
            dst_ref=piece(t, s),
            send_sem=send.at[t, way, s],
            recv_sem=recv.at[t, s],
            device_id={"seq": ways[way][1]},
            device_id_type=MESH,
        )

    def when(cond, act):
        if cond is None:
            act()
        else:
            pl.when(cond)(act)

    def fan(t, s, dirs, start):
        for way in dirs:
            c = copy(t, s, way)
            when(ways[way][0], c.start if start else c.wait_send)

    def arrive(t, s):
        copy(t, s, 4).wait_recv()

    def inside(i, size):
        return jnp.logical_and(i >= 0, i < size)

    def along_a(d, start):
        for t in range(PIECES):
            for sg in (1, -1):
                x = a + sg * d

                @pl.when(jnp.logical_and(inside(x, A), d < A))
                def _(x=x, sg=sg, t=t):
                    s = slot(x, b, core)
                    if start:
                        arrive(t, s)
                    fan(t, s, (1 if sg > 0 else 0, 2, 3, 4), start)

    def along_b(d, start):
        for e in range(1, B):
            for t in range(PIECES):
                for sg in (1, -1):
                    x = a + sg * d
                    ok = inside(x, A) if sg > 0 else jnp.logical_and(inside(x, A), d > 0)
                    for sb in (1, -1):
                        y = b + sb * e

                        @pl.when(jnp.logical_and(ok, inside(y, B)))
                        def _(x=x, y=y, sb=sb, t=t):
                            s = slot(x, y, core)
                            if start:
                                arrive(t, s)
                            fan(t, s, (3 if sb > 0 else 2, 4), start)

    barrier = pltpu.get_barrier_semaphore()

    def greet(i, _):
        pl.semaphore_signal(barrier, inc=1, device_id={"seq": lax.rem(me + i, n)}, device_id_type=MESH)
        return 0

    lax.fori_loop(1, n, greet, 0)
    k_load = pltpu.make_async_copy(k_hbm, kbuf.at[me], load.at[0])
    v_load = pltpu.make_async_copy(v_hbm, vbuf.at[me], load.at[1])
    q_load = pltpu.make_async_copy(q_hbm, q_ref, load.at[2])
    small = [
        pltpu.make_async_copy(src, dst, load.at[3 + i])
        for i, (src, dst) in enumerate((
            (order_hbm, order_ref), (qb_hbm, qb_ref), (kb_hbm, kb_ref), (vb_hbm, vb_ref), (tab_hbm, tab_ref),
        ))
    ]
    for c in small + [k_load, v_load, q_load]:
        c.start()

    lane = lax.broadcasted_iota(jnp.int32, (1, HEAD), 1)

    def placed(values):
        size = values.shape[1]
        spots = HEAD // size
        return jnp.where(lane // size == me % spots, jnp.concatenate([values] * spots, axis=1), 0.0)

    def row(ref):
        return ref[...].astype(jnp.float32)[None, :]

    for c in small:
        c.wait()
    pack_ref[...] = jnp.zeros_like(pack_ref)
    q_row = row(qb_ref)
    if qper >= HEAD:
        for i in range(qper // HEAD):
            pack_ref[i : i + 1, :] = q_row[:, i * HEAD : (i + 1) * HEAD]
    else:
        pack_ref[0:1, :] = placed(q_row)
    pack_ref[2:3, :] = placed(row(kb_ref))
    pack_ref[3:4, :] = placed(row(vb_ref))
    qpos = (lane % FRAME_TOK).astype(jnp.float32)
    for f in range(frames):
        frame = order_ref[f].astype(jnp.float32)
        pack_ref[8 - frames + f : 9 - frames + f, :] = jnp.full((1, HEAD), 1.0, jnp.float32) * frame
        qpos = qpos + jnp.where((lane % rows) // FRAME_TOK == f, frame * FRAME_TOK, 0.0)
    pbuf[me] = pack_ref[...]
    tab = tab_ref[...]
    q_cos, q_sin = cos_sin(pack_ref[8 - frames :, :], tab)
    fold = math.log2(math.e) / math.sqrt(HEAD)
    q_cos, q_sin = q_cos * fold, q_sin * fold
    k_load.wait()
    v_load.wait()
    pl.semaphore_wait(barrier, n - 1)

    def pack_copy(i, s):
        return pltpu.make_async_remote_copy(
            src_ref=pack_ref,
            dst_ref=pbuf.at[s],
            send_sem=psend.at[i],
            recv_sem=precv.at[s],
            device_id={"seq": lax.rem(me + i, n)},
            device_id_type=MESH,
        )

    def push(i, _):
        pack_copy(i, me).start()
        return 0

    lax.fori_loop(1, n, push, 0)
    for t in range(PIECES):
        fan(t, me, (0, 1, 2, 3, 4), True)

    acc[...] = jnp.zeros_like(acc)
    den[...] = jnp.zeros_like(den)
    top[...] = jnp.full_like(top, NEG)

    def pulled(i, _):
        pack_copy(i, lax.rem(me + i, n)).wait_recv()
        return 0

    lax.fori_loop(1, n, pulled, 0)
    q_load.wait()

    for h in range(QH):
        if qper >= HEAD:
            per = qper // HEAD
            bias = pbuf[h // per, h % per : h % per + 1, :]
        else:
            parts = HEAD // qper
            bias = sum(pbuf[h * parts + i, 0:1, :] for i in range(parts))
        x = q_ref[:, h * HEAD : (h + 1) * HEAD].astype(jnp.float32) + bias
        at = (h % RATIO) * rows
        qs[h // RATIO, at : at + rows, :] = spin(x, q_cos, q_sin).astype(jnp.bfloat16)
    share = n // KVH
    k_bias = [sum(pbuf[g * share + i, 2:3, :] for i in range(share)) for g in range(KVH)]
    v_bias = [sum(pbuf[g * share + i, 3:4, :] for i in range(share)) for g in range(KVH)]
    within = lax.broadcasted_iota(jnp.int32, (FRAME_TOK, HEAD), 0).astype(jnp.float32)

    def chunk(first):
        for j in range(4):
            s = first + j
            order = pbuf[s][8 - frames :, :]
            cosine, sine = cos_sin(order, tab)
            for f in range(frames):
                kpos = order[f : f + 1, :] * FRAME_TOK + within
                at = j * rows + f * FRAME_TOK
                hide[at : at + FRAME_TOK, :] = jnp.where(kpos <= qpos, 0.0, NEG)
            for g in range(KVH):
                cols = slice(g * HEAD, (g + 1) * HEAD)
                x = kbuf[s, :, cols].astype(jnp.float32) + k_bias[g]
                ksc[g, j * rows : (j + 1) * rows, :] = spin(x, cosine, sine).astype(jnp.bfloat16)
                y = vbuf[s, :, cols].astype(jnp.float32) + v_bias[g]
                vsc[g, j * rows : (j + 1) * rows, :] = y.astype(jnp.bfloat16)
        for g in range(KVH):
            scores = lax.dot_general(
                ksc[g], qs[g], (((1,), (1,)), ((), ())), preferred_element_type=jnp.float32
            )
            mask = hide[...]
            scores = scores + jnp.concatenate([mask] * (scores.shape[1] // HEAD), axis=1)
            old = top[g]
            new = jnp.maximum(old, jnp.max(scores, axis=0, keepdims=True))
            expo = jnp.exp2(scores - new)
            factor = jnp.exp2(old - new)
            top[g] = new
            den[g] = den[g] * factor + jnp.sum(expo, axis=0, keepdims=True)
            acc[g] = acc[g] * factor + lax.dot_general(
                vsc[g], expo.astype(jnp.bfloat16), (((0,), (0,)), ((), ())),
                preferred_element_type=jnp.float32,
            )

    low = a < A // 2
    mirror = jnp.where(low, a, A - 1 - a)

    def step(d, _):
        along_a(d + 1, True)
        along_b(d, True)
        near = jnp.where(d % 2 == 1, -((d + 1) // 2), d // 2)
        plane = mirror + jnp.where(d <= 2 * mirror, near, d - mirror)
        plane = jnp.where(low, plane, A - 1 - plane)
        for y in range(B):
            for t in range(PIECES):
                arrive(t, slot(plane, y, 1 - core))
        if 2 * B == 4:
            chunk(plane * 4)
        else:
            def part(i, _):
                chunk(plane * 2 * B + i * 4)
                return 0

            lax.fori_loop(0, 2 * B // 4, part, 0)
        return 0

    lax.fori_loop(0, A, step, 0)

    for g in range(KVH):
        mixed = acc[g] * (1.0 / den[g])
        flat = mixed.T.astype(jnp.bfloat16)
        for r in range(RATIO):
            h = g * RATIO + r
            o_ref[:, h * HEAD : (h + 1) * HEAD] = flat[r * rows : (r + 1) * rows, :]

    for t in range(PIECES):
        fan(t, me, (0, 1, 2, 3, 4), False)

    def drain(d, _):
        along_a(d + 1, False)
        along_b(d, False)
        return 0

    lax.fori_loop(0, A, drain, 0)

    def pushed(i, _):
        pack_copy(i, me).wait_send()
        return 0

    lax.fori_loop(1, n, pushed, 0)


UP, DOWN, ACROSS, SIDE = range(4)


def near_kernel(
    A, n, qper,
    q_hbm, k_hbm, v_hbm, qb_hbm, kb_hbm, vb_hbm, order_hbm, tab_hbm,
    o_ref,
    qb_ref, kb_ref, vb_ref, order_ref, tab_ref,
    q_ref, kbuf, vbuf, pbuf, cosb, sinb, qs, acc, top, den, fac, ksc, vsc, prob, hide,
    recv, send, precv, psend, zrecv, zsend, load, token,
):
    me = lax.axis_index("seq")
    rows = kbuf.shape[1]
    frames = rows // FRAME_TOK
    plane_size = 4
    core = me % 2
    b = (me // 2) % 2
    a = me // plane_size

    def slot(x, y, z):
        return (x * 2 + y) * 2 + z

    ways = (
        (a + 1 < A, slot(a + 1, b, core)),
        (a > 0, slot(a - 1, b, core)),
        (None, slot(a, 1 - b, core)),
        (None, slot(a, b, 1 - core)),
    )
    mates = (slot(a, b, 1 - core), slot(a, 1 - b, core), slot(a, 1 - b, 1 - core))

    def when(cond, act):
        if cond is None:
            act()
        else:
            pl.when(cond)(act)

    def both(one, two):
        return two if one is None else jnp.logical_and(one, two)

    def copy(t, s, way):
        piece = (kbuf, vbuf)[t].at[s]
        return pltpu.make_async_remote_copy(
            src_ref=piece, dst_ref=piece,
            send_sem=send.at[t, way, s], recv_sem=recv.at[t, s],
            device_id={"seq": ways[way][1]}, device_id_type=MESH,
        )

    def go(t, s, way):
        when(ways[way][0], copy(t, s, way).start)

    def arrive(t, s):
        copy(t, s, SIDE).wait_recv()

    def mate_copy(i, s):
        return pltpu.make_async_remote_copy(
            src_ref=pbuf.at[s], dst_ref=pbuf.at[s],
            send_sem=psend.at[i], recv_sem=precv.at[i],
            device_id={"seq": mates[i]}, device_id_type=MESH,
        )

    def far_copy(x, p):
        rows_of = pbuf.at[pl.ds(p * plane_size, plane_size)]
        return pltpu.make_async_remote_copy(
            src_ref=rows_of, dst_ref=rows_of,
            send_sem=zsend.at[x], recv_sem=zrecv.at[p],
            device_id={"seq": slot(x, b, core)}, device_id_type=MESH,
        )

    def inside(x):
        return jnp.logical_and(x >= 0, x < A)

    barrier = pltpu.get_barrier_semaphore()

    def greet(s):
        pl.semaphore_signal(barrier, inc=1, device_id={"seq": s}, device_id_type=MESH)

    for s in mates:
        greet(s)
    for way in (UP, DOWN):
        when(ways[way][0], functools.partial(greet, ways[way][1]))

    small = [
        pltpu.make_async_copy(src, dst, load.at[3 + i])
        for i, (src, dst) in enumerate((
            (order_hbm, order_ref), (qb_hbm, qb_ref), (kb_hbm, kb_ref), (vb_hbm, vb_ref), (tab_hbm, tab_ref),
        ))
    ]
    k_load = pltpu.make_async_copy(k_hbm, kbuf.at[me], load.at[0])
    v_load = pltpu.make_async_copy(v_hbm, vbuf.at[me], load.at[1])
    q_load = pltpu.make_async_copy(q_hbm, q_ref, load.at[2])
    for c in small + [k_load, v_load, q_load]:
        c.start()

    lane = lax.broadcasted_iota(jnp.int32, (1, HEAD), 1)

    def placed(values):
        spots = HEAD // values.shape[1]
        return jnp.where(lane // values.shape[1] == me % spots, jnp.concatenate([values] * spots, axis=1), 0.0)

    def row(ref):
        return ref[...].astype(jnp.float32)[None, :]

    for c in small:
        c.wait()
    per = qper // HEAD
    q_row = row(qb_ref)
    parts = [q_row[:, i * HEAD : (i + 1) * HEAD] for i in range(per)]
    parts += [jnp.zeros((1, HEAD), jnp.float32)] * (2 - per)
    parts += [placed(row(kb_ref)), placed(row(vb_ref))]
    qpos = (lane % FRAME_TOK).astype(jnp.float32)
    for f in range(frames):
        frame = order_ref[f].astype(jnp.float32)
        parts.append(jnp.full((1, HEAD), 1.0, jnp.float32) * frame)
        qpos = qpos + jnp.where((lane % rows) // FRAME_TOK == f, frame * FRAME_TOK, 0.0)
    pbuf[me] = jnp.concatenate(parts, axis=0)
    k_load.wait()
    v_load.wait()
    count = 3 + (a + 1 < A).astype(jnp.int32) + (a > 0).astype(jnp.int32)
    pl.semaphore_wait(barrier, count)

    for i in range(3):
        mate_copy(i, me).start()
    for t in range(2):
        for way in (ACROSS, UP, DOWN, SIDE):
            go(t, me, way)

    def tell(way, sg, k):
        ahead = a + sg * k

        def act():
            pl.semaphore_signal(
                token.at[way], inc=1, device_id={"seq": slot(a - sg, b, core)}, device_id_type=MESH
            )

        pl.when(jnp.logical_and(inside(ahead), inside(a - sg)))(act)

    for way, sg in ((UP, 1), (DOWN, -1)):
        tell(way, sg, 1)
    acc[...] = jnp.zeros_like(acc)
    den[...] = jnp.zeros_like(den)
    top[...] = jnp.full_like(top, NEG)
    tab = tab_ref[...]
    fold = math.log2(math.e) / math.sqrt(HEAD)
    q_cos, q_sin = cos_sin(pbuf[me][8 - frames :, :], tab)
    q_cos, q_sin = q_cos * fold, q_sin * fold
    for k in range(2, A):
        for way, sg in ((UP, 1), (DOWN, -1)):
            @pl.when(inside(a + sg * k))
            def _(way=way):
                pl.semaphore_wait(token.at[way], 1)

            tell(way, sg, k)
    for i in range(3):
        mate_copy(i, mates[i]).wait_recv()
    for k in range(1, A):
        for sg in (1, -1):
            x = a + sg * k
            pl.when(inside(x))(lambda x=x: far_copy(x, a).start())

    low = a < A // 2
    mirror = jnp.where(low, a, A - 1 - a)

    def plane_at(d):
        near = -((d + 1) // 2) if d % 2 == 1 else d // 2
        p = mirror + jnp.where(d <= 2 * mirror, near, d - mirror)
        return jnp.where(low, p, A - 1 - p)

    def along(d, t):
        for sg in (1, -1):
            x = a + sg * d

            @pl.when(inside(x))
            def _(x=x, sg=sg):
                s = slot(x, b, core)
                arrive(t, s)
                go(t, s, DOWN if sg > 0 else UP)
                go(t, s, ACROSS)
                go(t, s, SIDE)

    def crossed(p, t):
        s = slot(p, 1 - b, core)
        arrive(t, s)
        go(t, s, SIDE)

    def beside(p, t):
        for y in range(2):
            arrive(t, slot(p, y, 1 - core))

    planes = [plane_at(d) for d in range(A)]

    def event(j):
        d, t = j // 2, j % 2
        if d + 1 < A:
            along(d + 1, t)
        if d < A:
            crossed(planes[d], t)

    event(0)
    event(1)
    q_load.wait()
    for x in range(A):
        pl.when(x != a)(lambda x=x: far_copy(0, x).wait_recv())

    everyone = pbuf[...].reshape(n * 8, HEAD)
    angle = everyone * tab[32:33, :]
    turns = jnp.round(angle * (1.0 / (2.0 * math.pi)))
    angle = angle - turns * 6.28125
    angle = angle - turns * (2.0 * math.pi - 6.28125)
    sign = jnp.where(lane < HALF, -1.0, 1.0)
    cosb[...] = jnp.cos(angle).reshape(n, 8, HEAD)
    sinb[...] = (jnp.sin(angle) * sign).reshape(n, 8, HEAD)

    for h in range(QH):
        bias = pbuf[h // per, h % per : h % per + 1, :]
        x = q_ref[:, h * HEAD : (h + 1) * HEAD].astype(jnp.float32) + bias
        at = (h % RATIO) * rows
        qs[h // RATIO, at : at + rows, :] = spin(x, q_cos, q_sin).astype(jnp.bfloat16)
    share = n // KVH
    k_bias = [sum(pbuf[g * share + i, 2:3, :] for i in range(share)) for g in range(KVH)]
    v_bias = [sum(pbuf[g * share + i, 3:4, :] for i in range(share)) for g in range(KVH)]
    within = lax.broadcasted_iota(jnp.int32, (FRAME_TOK, HEAD), 0).astype(jnp.float32)
    temporal = lax.broadcasted_iota(jnp.int32, (FRAME_TOK, HEAD), 1) % HALF < PAIRS_T

    def score(p):
        for j in range(plane_size):
            s = p * plane_size + j
            order, cos_t, sin_t = pbuf[s], cosb[s], sinb[s]
            cosine, sine = [], []
            for f in range(frames):
                r = 8 - frames + f
                kpos = order[r : r + 1, :] * FRAME_TOK + within
                at = j * rows + f * FRAME_TOK
                hide[at : at + FRAME_TOK, :] = jnp.where(kpos <= qpos, 0.0, NEG)
                cosine.append(jnp.where(temporal, cos_t[r : r + 1, :], tab[0:16, :]))
                sine.append(jnp.where(temporal, sin_t[r : r + 1, :], tab[16:32, :]))
            cosine, sine = jnp.concatenate(cosine, axis=0), jnp.concatenate(sine, axis=0)
            for g in range(KVH):
                x = kbuf[s, :, g * HEAD : (g + 1) * HEAD].astype(jnp.float32) + k_bias[g]
                ksc[g, j * rows : (j + 1) * rows, :] = spin(x, cosine, sine).astype(jnp.bfloat16)
        for g in range(KVH):
            scores = lax.dot_general(
                ksc[g], qs[g], (((1,), (1,)), ((), ())), preferred_element_type=jnp.float32
            )
            mask = hide[...]
            scores = scores + jnp.concatenate([mask] * (scores.shape[1] // HEAD), axis=1)
            old = top[g]
            new = jnp.maximum(old, jnp.max(scores, axis=0, keepdims=True))
            expo = jnp.exp2(scores - new)
            factor = jnp.exp2(old - new)
            top[g] = new
            fac[g] = factor
            den[g] = den[g] * factor + jnp.sum(expo, axis=0, keepdims=True)
            prob[g] = expo.astype(jnp.bfloat16)

    def mix(p):
        for j in range(plane_size):
            s = p * plane_size + j
            for g in range(KVH):
                y = vbuf[s, :, g * HEAD : (g + 1) * HEAD].astype(jnp.float32) + v_bias[g]
                vsc[g, j * rows : (j + 1) * rows, :] = y.astype(jnp.bfloat16)
        for g in range(KVH):
            acc[g] = acc[g] * fac[g] + lax.dot_general(
                vsc[g], prob[g], (((0,), (0,)), ((), ())), preferred_element_type=jnp.float32,
            )

    last = 2 * A
    nxt = 2
    event(nxt)
    nxt += 1
    for d in range(A):
        p = planes[d]
        while d == A - 1 and nxt < last:
            event(nxt)
            nxt += 1
        beside(p, 0)
        score(p)
        if nxt < last - 1:
            event(nxt)
            nxt += 1
        beside(p, 1)
        mix(p)
        if nxt < last - 1:
            event(nxt)
            nxt += 1

    for g in range(KVH):
        mixed = acc[g] * (1.0 / den[g])
        flat = mixed.T.astype(jnp.bfloat16)
        for r in range(RATIO):
            h = g * RATIO + r
            o_ref[:, h * HEAD : (h + 1) * HEAD] = flat[r * rows : (r + 1) * rows, :]

    for i in range(3):
        mate_copy(i, me).wait_send()
    for k in range(1, A):
        for sg in (1, -1):
            x = a + sg * k
            pl.when(inside(x))(lambda x=x: far_copy(x, a).wait_send())
    for t in range(2):
        for way in range(4):
            when(ways[way][0], copy(t, me, way).wait_send)
        for d in range(1, A):
            for sg in (1, -1):
                x = a + sg * d

                @pl.when(inside(x))
                def _(x=x, sg=sg, t=t):
                    s = slot(x, b, core)
                    way = DOWN if sg > 0 else UP
                    when(ways[way][0], copy(t, s, way).wait_send)
                    copy(t, s, ACROSS).wait_send()
                    copy(t, s, SIDE).wait_send()

        for p in planes:
            copy(t, slot(p, 1 - b, core), SIDE).wait_send()


def near_call(A, n, qper, *operands):
    query, keys, query_bias, key_bias, frame_order = (operands[i] for i in (0, 1, 3, 4, 6))
    rows = keys.shape[0]
    wide = RATIO * rows
    deep = 4 * rows
    whole = pl.BlockSpec(memory_space=pltpu.VMEM)
    far = pl.BlockSpec(memory_space=pltpu.HBM)
    return pl.pallas_call(
        functools.partial(near_kernel, A, n, qper),
        out_shape=jax.ShapeDtypeStruct(query.shape, jnp.bfloat16),
        in_specs=[far] * 8,
        out_specs=whole,
        scratch_shapes=[
            pltpu.VMEM(query_bias.shape, jnp.bfloat16),
            pltpu.VMEM(key_bias.shape, jnp.bfloat16),
            pltpu.VMEM(key_bias.shape, jnp.bfloat16),
            pltpu.SMEM(frame_order.shape, jnp.int32),
            pltpu.VMEM((40, HEAD), jnp.float32),
            pltpu.VMEM(query.shape, jnp.bfloat16),
            pltpu.VMEM((n, rows, KVH * HEAD), jnp.bfloat16),
            pltpu.VMEM((n, rows, KVH * HEAD), jnp.bfloat16),
            pltpu.VMEM((n, 8, HEAD), jnp.float32),
            pltpu.VMEM((n, 8, HEAD), jnp.float32),
            pltpu.VMEM((n, 8, HEAD), jnp.float32),
            pltpu.VMEM((KVH, wide, HEAD), jnp.bfloat16),
            pltpu.VMEM((KVH, HEAD, wide), jnp.float32),
            pltpu.VMEM((KVH, 1, wide), jnp.float32),
            pltpu.VMEM((KVH, 1, wide), jnp.float32),
            pltpu.VMEM((KVH, 1, wide), jnp.float32),
            pltpu.VMEM((KVH, deep, HEAD), jnp.bfloat16),
            pltpu.VMEM((KVH, deep, HEAD), jnp.bfloat16),
            pltpu.VMEM((KVH, deep, wide), jnp.bfloat16),
            pltpu.VMEM((deep, HEAD), jnp.float32),
            pltpu.SemaphoreType.DMA((2, n)),
            pltpu.SemaphoreType.DMA((2, 4, n)),
            pltpu.SemaphoreType.DMA((3,)),
            pltpu.SemaphoreType.DMA((3,)),
            pltpu.SemaphoreType.DMA((A,)),
            pltpu.SemaphoreType.DMA((A,)),
            pltpu.SemaphoreType.DMA((8,)),
            pltpu.SemaphoreType.REGULAR((2,)),
        ],
        compiler_params=pltpu.CompilerParams(vmem_limit_bytes=24 << 20, collective_id=0, has_side_effects=True),
    )(*(
        pltpu.with_memory_space_constraint(x, pltpu.HBM)
        for x in operands + (jnp.asarray(tables()),)
    ))


def on_device(n, query, keys, values, query_bias, key_bias, value_projection_bias, frame_order):
    chips = n // 2
    B = 1
    while B * B * 4 <= chips:
        B *= 2
    A = chips // B
    rows = keys.shape[0]
    qper = query_bias.shape[0]
    if B == 2 and qper >= HEAD:
        return near_call(A, n, qper, query, keys, values, query_bias, key_bias, value_projection_bias, frame_order)
    wide = RATIO * rows
    keys_at_once = 4 * rows
    whole = pl.BlockSpec(memory_space=pltpu.VMEM)
    far = pl.BlockSpec(memory_space=pltpu.HBM)
    return pl.pallas_call(
        functools.partial(kernel, A, B, n, qper),
        out_shape=jax.ShapeDtypeStruct(query.shape, jnp.bfloat16),
        in_specs=[far] * 8,
        out_specs=whole,
        scratch_shapes=[
            pltpu.VMEM(query_bias.shape, jnp.bfloat16),
            pltpu.VMEM(key_bias.shape, jnp.bfloat16),
            pltpu.VMEM(key_bias.shape, jnp.bfloat16),
            pltpu.SMEM(frame_order.shape, jnp.int32),
            pltpu.VMEM((40, HEAD), jnp.float32),
            pltpu.VMEM(query.shape, jnp.bfloat16),
            pltpu.VMEM((8, HEAD), jnp.float32),
            pltpu.VMEM((n, rows, KVH * HEAD), jnp.bfloat16),
            pltpu.VMEM((n, rows, KVH * HEAD), jnp.bfloat16),
            pltpu.VMEM((n, 8, HEAD), jnp.float32),
            pltpu.VMEM((KVH, wide, HEAD), jnp.bfloat16),
            pltpu.VMEM((KVH, HEAD, wide), jnp.float32),
            pltpu.VMEM((KVH, 1, wide), jnp.float32),
            pltpu.VMEM((KVH, 1, wide), jnp.float32),
            pltpu.VMEM((KVH, keys_at_once, HEAD), jnp.bfloat16),
            pltpu.VMEM((KVH, keys_at_once, HEAD), jnp.bfloat16),
            pltpu.VMEM((keys_at_once, HEAD), jnp.float32),
            pltpu.SemaphoreType.DMA((PIECES, n)),
            pltpu.SemaphoreType.DMA((PIECES, 5, n)),
            pltpu.SemaphoreType.DMA((n,)),
            pltpu.SemaphoreType.DMA((n,)),
            pltpu.SemaphoreType.DMA((8,)),
        ],
        compiler_params=pltpu.CompilerParams(vmem_limit_bytes=(16 if n <= 32 else 48) << 20, collective_id=0, has_side_effects=True),
    )(*(
        pltpu.with_memory_space_constraint(x, pltpu.HBM)
        for x in (
            query, keys, values, query_bias, key_bias, value_projection_bias, frame_order,
            jnp.asarray(tables()),
        )
    ))


def solution(mesh):
    placed = (
        P(("groups", "seq"), None),
        P(("groups", "seq"), None),
        P(("groups", "seq"), None),
        P("seq"),
        P("seq"),
        P("seq"),
        P(("groups", "seq")),
    )
    return jax.shard_map(
        functools.partial(on_device, mesh.shape["seq"]),
        mesh=mesh,
        in_specs=placed,
        out_specs=P(("groups", "seq"), None),
        check_vma=False,
    )
```
